128 devices in a mesh: row: 32 (over z, x, core), blk: 4 (over y).
Axes of the slice: x: 4, y: 4, z: 4, core: 2. Of those that a mesh axis runs over, the one named last changes fastest.
Arguments:
- g_wannier: bfloat16 [512, 2, 512, 1024], P('row', None, None, 'blk'), may hold values from -0.03125 to 0.03125
- k_angle: float32 [256, 512], replicated, may hold values from -3.140625 to 3.140625
- q_angle: float32 [128, 512], replicated, may hold values from -3.140625 to 3.140625
- eig_k: bfloat16 [256, 2, 32, 32], P('row'), may hold values from -0.75 to 0.75
- eig_kq: bfloat16 [2048, 2, 32, 32], P(('row', 'blk')), may hold values from -0.75 to 0.75
- mask_k: int32 [256, 32], P('row'), may hold values 0 or 1
- mask_kq: int32 [2048, 32], P(('row', 'blk')), may hold values 0 or 1
- owner: int32 [4, 256, 32, 1], P('blk', 'row'), may hold values from 0 to 127; in each aligned block of 256 rows (0 to 255, 256 to 511, ..., all dimensions but the last counted through in order) at most 4 rows name the same one
- kq_local: int32 [4, 256, 32, 1], P('blk', 'row'), may hold values from 0 to 15
Outputs:
- couplings: bfloat16 [128, 256, 1024], P('blk', 'row')
The draws below stay inside these ranges and needn't reach their ends.
Inputs may be any that keep to these rules, and one draw needn't show every extreme that they name: Within the pairs of one device (aligned blocks of 256 rows of the flattened leading dimensions) no owner is named more than 4 times, a bound that some block reaches.
All inputs are finite; a program needn't handle non-finite values. No bound on the sum of `mask_k` or of `mask_kq` on one device may be relied on, other than what follows from the above.
Results may differ from the reference program's by a relative error of at most 0.0073.
Values may be sent and summed in bfloat16 or wider, within the bound.
No kernel may reach another device: no remote copies, remote signals or barrier semaphores. Data moves between devices by JAX's collectives and lax.ppermute only.
A program may use at most 128 MiB of HBM per device.

```python
import math
import jax
import jax.numpy as jnp
import numpy as np
from jax import lax

NB = 32
RE = 512
RP = 512
K_DEV = 8
QD = 32
K = 256
Q = 128
CAP = 4
KQ_DEV = 16
KQ = 2048
N_BLK = 4
DEVICES = 128


def touch_ends(entries, key, least, top_value):
    index_at = [jax.random.randint(jax.random.fold_in(key, axis), (), 0, length) for axis, length in enumerate(entries.shape)]
    main_axis = entries.shape.index(max(entries.shape))
    beside = index_at[:main_axis] + [(index_at[main_axis] + 1) % entries.shape[main_axis]] + index_at[main_axis + 1:]
    return entries.at[tuple(index_at)].set(least).at[tuple(beside)].set(top_value)


def levels(own_key, dims, cuts, low, high):
    def one(axis_at, blocks):
        steps = jax.random.uniform(jax.random.fold_in(jax.random.fold_in(own_key, 6), axis_at), (blocks,), jnp.float32, low / len(cuts), high / len(cuts))
        return jnp.repeat(jnp.exp(steps), dims[axis_at] // blocks).reshape((-1,) + (1,) * (len(dims) - axis_at - 1))

    factor_of = one(*cuts[0])
    for cut in cuts[1:]:
        factor_of = factor_of * one(*cut)
    return factor_of


def routed_block(key, own, number, rows, number_of, top, reach, skew):
    order = jax.random.permutation(key, number_of)
    packed, common = load_shares(number_of, rows * top, reach, skew, True), load_shares(number_of, rows * top, reach, skew, False)
    places = jnp.arange(number_of)

    def named(lengths, turn):
        used = int((lengths > 0).sum())
        fixed = max(1, used // 4)
        shifted = fixed + (places - fixed + turn * (used - fixed)) % max(1, number_of - fixed)
        return jnp.zeros((number_of,), jnp.int32).at[order[jnp.where(places < fixed, places, shifted)]].set(jnp.asarray(lengths, jnp.int32))

    lengths = jnp.where(number % 4 == 0, named(packed, number // 4), named(common, number - number // 4 - 1))
    mixed = jax.random.permutation(jax.random.fold_in(own, 3), number_of)
    source_of, taker = mixed[0:number_of // 2 * 2:2], mixed[1:number_of // 2 * 2:2]
    room = jnp.minimum(lengths[source_of] - 1, reach - lengths[taker]) // 2
    room = jnp.where((source_of == order[0]) | (taker == order[0]) | (lengths[taker] == 0), 0, jnp.maximum(room, 0))
    shifted = jax.random.randint(jax.random.fold_in(own, 4), (number_of // 2,), 0, 1 << 20) % (room + 1)
    lengths = lengths.at[source_of].add(-shifted).at[taker].add(shifted)
    labels = jnp.searchsorted(jnp.cumsum(lengths), jnp.arange(rows * top), side="right").astype(jnp.int32)
    grid = labels.reshape(top, rows).T
    grid = grid[jax.random.permutation(jax.random.fold_in(own, 1), rows)]
    turn = jax.random.randint(jax.random.fold_in(own, 2), (rows, 1), 0, top)
    return jnp.take_along_axis(grid, (jnp.arange(top)[None, :] + turn) % top, axis=1)


def load_shares(count, total, bound, slope, full):
    weights = [(1 << 20) // math.isqrt(rank ** slope) + 1 for rank in range(1, count + 1)]
    largest = bound if full else min(bound, max(-(-total // count), total * weights[0] // sum(weights)))
    least = 1 if total - largest >= count - 1 else 0
    given, spare = [largest] + [least] * (count - 1), total - largest - least * (count - 1)
    while spare > 0:
        candidates = [i for i in range(1, count) if given[i] < largest] or [i for i in range(1, count) if given[i] < bound]
        whole, left = sum([weights[i] for i in candidates]), spare
        for i in candidates:
            extra = min(bound - given[i], max(1, left * weights[i] // whole), spare)
            given[i] = given[i] + extra
            spare = spare - extra
    return np.array(given)


def gaussian(stream_key, shape, width, limit, pieces=(), kind=jnp.bfloat16):
    result = width * jax.random.normal(stream_key, shape, jnp.float32)
    if pieces:
        result = result * levels(stream_key, shape, pieces, -0.22, 0.18)
    return jnp.clip(result, -limit, limit).astype(kind)


def setup_inputs(seed: int = 0) -> dict:
    keys = jax.random.split(jax.random.key(seed), 10)
    g_wannier = gaussian(keys[0], (RP, 2, RE, NB * NB), ((RE * RP) ** -0.5), 0.03125, ((0, 32), (3, 4)))
    k_angle = jnp.clip(jax.random.uniform(keys[1], (K, RE), jnp.float32, -3.140625, 3.140625), -3.140625, 3.140625)
    q_angle = jnp.clip(jax.random.uniform(keys[2], (Q, RP), jnp.float32, -3.140625, 3.140625), -3.140625, 3.140625)
    eig_k = gaussian(keys[3], (K, 2, NB, NB), (2 * NB) ** -0.5, 0.75, ((0, 32),))
    eig_kq = gaussian(keys[4], (KQ, 2, NB, NB), (2 * NB) ** -0.5, 0.75, ((0, 128),))
    mask_k = touch_ends((jax.random.randint(keys[5], (K, NB), 0, 4) < 3).astype(jnp.int32), jax.random.fold_in(keys[5], 1), 0, 1)
    mask_kq = touch_ends((jax.random.randint(keys[6], (KQ, NB), 0, 4) < 3).astype(jnp.int32), jax.random.fold_in(keys[6], 1), 0, 1)
    owner_keys = jax.random.split(jax.random.fold_in(keys[7], 1), N_BLK * K * QD // (K_DEV * QD))
    owner_turns = jax.random.permutation(jax.random.fold_in(keys[7], 3), N_BLK * K * QD // (K_DEV * QD))
    owner = jax.vmap(lambda own, number: routed_block(jax.random.fold_in(keys[7], 2), own, number, K_DEV * QD, DEVICES, 1, CAP, 2))(owner_keys, owner_turns).reshape((N_BLK, K, QD, 1))
    kq_local = touch_ends(jax.random.randint(keys[8], (N_BLK, K, QD, 1), 0, KQ_DEV), jax.random.fold_in(keys[8], 1), 0, KQ_DEV - 1).astype(jnp.int32)
    return {"g_wannier": g_wannier, "k_angle": k_angle, "q_angle": q_angle, "eig_k": eig_k, "eig_kq": eig_kq, "mask_k": mask_k, "mask_kq": mask_kq, "owner": owner, "kq_local": kq_local}


def reference(g_wannier, k_angle, q_angle, eig_k, eig_kq, mask_k, mask_kq, owner, kq_local):
    stacked = jnp.transpose(g_wannier.reshape(RP, 2 * RE, NB * NB), (1, 0, 2)).reshape(2 * RE, RP * NB * NB)
    k_cos = jnp.cos(k_angle).astype(jnp.bfloat16)
    k_sin = jnp.sin(k_angle).astype(jnp.bfloat16)
    q_cos = jnp.cos(q_angle).astype(jnp.bfloat16)
    q_sin = jnp.sin(q_angle).astype(jnp.bfloat16)
    q_phase = jnp.concatenate([jnp.concatenate([q_cos, -q_sin], 1), jnp.concatenate([q_sin, q_cos], 1)], 0)
    masked_k = eig_k * mask_k.astype(jnp.bfloat16)[:, None, None, :]
    masked_kq = eig_kq * mask_kq.astype(jnp.bfloat16)[:, None, None, :]
    point = (owner[..., 0] * KQ_DEV + kq_local[..., 0]).astype(jnp.int32)
    point = jnp.transpose(point, (0, 2, 1)).reshape(Q, K)

    def one_block(first_k):
        cos_rows = lax.dynamic_slice_in_dim(k_cos, first_k, K_DEV, 0)
        sin_rows = lax.dynamic_slice_in_dim(k_sin, first_k, K_DEV, 0)
        k_phase = jnp.concatenate([jnp.concatenate([cos_rows, -sin_rows], 1), jnp.concatenate([sin_rows, cos_rows], 1)], 0)
        k_part = jnp.dot(k_phase, stacked, preferred_element_type=jnp.float32).astype(jnp.bfloat16)
        k_part = jnp.transpose(k_part.reshape(2, K_DEV, RP, NB * NB), (0, 2, 1, 3)).reshape(2 * RP, K_DEV * NB * NB)
        q_part = jnp.dot(q_phase, k_part, preferred_element_type=jnp.float32).astype(jnp.bfloat16)
        q_part = q_part.reshape(2, Q, K_DEV, NB, NB).astype(jnp.float32)
        rows_k = lax.dynamic_slice_in_dim(masked_k, first_k, K_DEV, 0).astype(jnp.float32)
        half_real = jnp.einsum("qkij,kjn->qkin", q_part[0], rows_k[:, 0]) - jnp.einsum("qkij,kjn->qkin", q_part[1], rows_k[:, 1])
        half_imag = jnp.einsum("qkij,kjn->qkin", q_part[0], rows_k[:, 1]) + jnp.einsum("qkij,kjn->qkin", q_part[1], rows_k[:, 0])
        half_real = lax.optimization_barrier(half_real.astype(jnp.bfloat16)).astype(jnp.float32)
        half_imag = lax.optimization_barrier(half_imag.astype(jnp.bfloat16)).astype(jnp.float32)
        points = lax.dynamic_slice_in_dim(point, first_k, K_DEV, 1)
        vectors = masked_kq[points].astype(jnp.float32)
        rot_real = jnp.einsum("qkim,qkin->qkmn", vectors[:, :, 0], half_real) + jnp.einsum("qkim,qkin->qkmn", vectors[:, :, 1], half_imag)
        rot_imag = jnp.einsum("qkim,qkin->qkmn", vectors[:, :, 0], half_imag) - jnp.einsum("qkim,qkin->qkmn", vectors[:, :, 1], half_real)
        squared = rot_real * rot_real + rot_imag * rot_imag
        return squared.astype(jnp.bfloat16).reshape(Q, K_DEV, NB * NB)

    starts = jnp.arange(K // K_DEV, dtype=jnp.int32) * K_DEV
    blocks = lax.map(one_block, starts)
    return jnp.transpose(blocks, (1, 0, 2, 3)).reshape(Q, K, NB * NB)
```

```python
import functools

import jax
import jax.numpy as jnp
import numpy as np
from jax import lax
from jax.experimental import pallas as pl
from jax.experimental.pallas import tpu as pltpu
from jax.sharding import PartitionSpec as P


F32 = jnp.float32
BF16 = jnp.bfloat16
VMEM = pltpu.VMEM
SMEM = pltpu.SMEM


def fitted(fun, odd):
    top = 3.15**2
    nodes = 0.5 * top * (1 - np.cos(np.pi * (np.arange(64) + 0.5) / 64))
    root = np.sqrt(nodes)
    values = fun(root) / root if odd else fun(root)
    cheb = np.polynomial.chebyshev.Chebyshev.fit(nodes, values, 8, domain=[0, top])
    return [float(v) for v in cheb.convert(kind=np.polynomial.Polynomial).coef]


SIN_COEF = fitted(np.sin, True)
COS_COEF = fitted(np.cos, False)


def cos_sin(angle):
    square = angle * angle

    def horner(coef):
        total = jnp.full_like(square, coef[-1])
        for c in coef[-2::-1]:
            total = total * square + c
        return total

    return horner(COS_COEF), horner(SIN_COEF) * angle


def row_id(z, x, c):
    return ((z % 4) * 4 + x % 4) * 2 + c % 2


def row_shift(value, dz=0, dx=0, dc=0):
    pairs = [
        (row_id(z, x, c), row_id(z + dz, x + dx, c + dc))
        for z in range(4)
        for x in range(4)
        for c in range(2)
    ]
    return lax.ppermute(value, "row", pairs)


def blk_shift(value, dy):
    return lax.ppermute(value, "blk", [(y, (y + dy) % 4) for y in range(4)])


def k_kernel(par, dest_ref, ang_ref, g_ref, *refs):
    outs, (phase, total, angle) = refs[:8], refs[8:]
    rp = pl.program_id(0)

    @pl.when(rp == 0)
    def _():
        for j in range(4):
            at = slice(j * 128, j * 128 + 128)
            right = slice(512 + j * 128, 640 + j * 128)
            angle[...] = ang_ref[:, at]
            cos, sin = cos_sin(angle[pl.ds(par, 128, stride=2), :])
            cos = cos.astype(BF16)
            sin = sin.astype(BF16)
            phase[0:128, at] = cos
            phase[0:128, right] = -sin
            phase[128:256, at] = sin
            phase[128:256, right] = cos

    part = jnp.dot(phase[...], g_ref[...].reshape(1024, 256), preferred_element_type=F32)
    total[0, pl.ds(rp, 256, stride=16), :] = part[:, 0:128]
    total[1, pl.ds(rp, 256, stride=16), :] = part[:, 128:256]

    @pl.when(rp == pl.num_programs(0) - 1)
    def _():
        for a in range(8):

            def one(inner, carry, a=a):
                dest = dest_ref[a * 4 + inner]
                for c in range(2):
                    for kk in range(4):
                        at = pl.multiple_of(((c * 32 + dest) * 4 + kk) * 16, 16)
                        for h in range(2):
                            block = total[h, pl.ds(at, 16), :].astype(BF16)
                            outs[a][inner, c, kk, :, h * 128 : h * 128 + 128] = block
                return carry

            lax.fori_loop(0, 4, one, 0)


def k_transform(par, dests, k_angle, g):
    out = jax.ShapeDtypeStruct((4, 2, 4, 16, 256), BF16)
    return pl.pallas_call(
        functools.partial(k_kernel, par),
        grid=(16,),
        in_specs=[
            pl.BlockSpec(memory_space=SMEM),
            pl.BlockSpec((256, 512), lambda r: (0, 0)),
            pl.BlockSpec((None, 2, 512, 256), lambda r: (r, 0, 0, 0)),
        ],
        out_specs=[pl.BlockSpec((4, 2, 4, 16, 256), lambda r: (0, 0, 0, 0, 0))] * 8,
        out_shape=[out] * 8,
        scratch_shapes=[
            VMEM((256, 1024), BF16),
            VMEM((2, 4096, 128), F32),
            VMEM((256, 128), F32),
        ],
        cost_estimate=pl.CostEstimate(
            flops=2 * 16 * 256 * 1024 * 256, bytes_accessed=10 << 20, transcendentals=0
        ),
        name=f"k_transform_{par}",
    )(dests, k_angle, g)


def prep_kernel(me_ref, q_ref, eig_ref, mask_ref, phase_out, eig_out):
    z, x, c, b = me_ref[0], me_ref[1], me_ref[2], me_ref[3]
    lane = lax.broadcasted_iota(jnp.int32, (32, 128), 1)
    for bd in range(4):
        for zd in range(4):
            rows = pl.ds(pl.multiple_of(lax.rem(b + bd, 4) * 32, 32), 32)
            cols = pl.ds(pl.multiple_of(lax.rem(z + zd, 4) * 128, 128), 128)
            ang = q_ref[rows, cols]
            ang = pltpu.roll(ang, lax.rem(128 - 32 * x, 128), 1)
            swapped = jnp.where(lane % 32 < 16, pltpu.roll(ang, 112, 1), pltpu.roll(ang, 16, 1))
            ang = jnp.where(c == 1, swapped, ang)
            cos, sin = cos_sin(ang)
            cos = cos.astype(BF16)
            sin = sin.astype(BF16)
            top = slice(bd * 32, bd * 32 + 32)
            low = slice(128 + bd * 32, 128 + bd * 32 + 32)
            left = slice(zd * 128, zd * 128 + 128)
            right = slice(512 + zd * 128, 512 + zd * 128 + 128)
            phase_out[top, left] = cos
            phase_out[top, right] = -sin
            phase_out[low, left] = sin
            phase_out[low, right] = cos
    for k in range(8):
        mask = mask_ref[k : k + 1, :].astype(F32)
        er = eig_ref[k, 0].astype(F32) * mask
        ei = eig_ref[k, 1].astype(F32) * mask
        first = [er, ei, er, ei, ei, -er, ei, -er]
        second = [-ei, er, -ei, er, er, ei, er, ei]
        eig_out[k, 0:32] = jnp.concatenate(first, 1).astype(BF16)
        eig_out[k, 32:64] = jnp.concatenate(second, 1).astype(BF16)


def prep(me, q_angle, eig_k, mask_k):
    whole = pl.BlockSpec(memory_space=VMEM)
    return pl.pallas_call(
        prep_kernel,
        in_specs=[pl.BlockSpec(memory_space=SMEM), whole, whole, whole],
        out_specs=[whole, whole],
        out_shape=[
            jax.ShapeDtypeStruct((256, 1024), BF16),
            jax.ShapeDtypeStruct((8, 64, 256), BF16),
        ],
        cost_estimate=pl.CostEstimate(flops=1 << 22, bytes_accessed=1 << 20, transcendentals=0),
        name="prep",
    )(me, q_angle, eig_k, mask_k)


def table_kernel(eig_ref, mask_ref, out_ref):
    for p in range(16):
        mask = mask_ref[p : p + 1, :].astype(F32)
        both = jnp.concatenate([eig_ref[p, 0], eig_ref[p, 1]], 0).astype(F32) * mask
        turned = jnp.transpose(both)
        out_ref[p] = jnp.concatenate([turned[0:16], turned[16:32]], 1).astype(BF16)


def table_of(eig_kq, mask_kq):
    whole = pl.BlockSpec(memory_space=VMEM)
    return pl.pallas_call(
        table_kernel,
        in_specs=[whole, whole],
        out_specs=whole,
        out_shape=jax.ShapeDtypeStruct((16, 16, 128), BF16),
        cost_estimate=pl.CostEstimate(flops=1 << 20, bytes_accessed=1 << 18, transcendentals=0),
        name="table",
    )(eig_kq, mask_kq)


def pick_kernel(idx_ref, *refs):
    parts, out_ref, table, sems = refs[:10], refs[10], refs[11], refs[12]
    copies = []
    for cd in range(2):
        own, y1, y3, y2a, y2b = parts[cd * 5 : cd * 5 + 5]
        at = cd * 1024
        for ref, start, size in (
            (own, at, 256),
            (y1, at + 256, 256),
            (y2a, at + 512, 128),
            (y2b, at + 640, 128),
            (y3, at + 768, 256),
        ):
            copies.append(
                pltpu.make_async_copy(ref, table.at[pl.ds(start, size)], sems.at[len(copies)])
            )
    for copy in copies:
        copy.start()
    for copy in copies:
        copy.wait()
    lane = lax.broadcasted_iota(jnp.int32, (16, 128), 1)
    low = lane < 64
    for k in range(8):

        def some(step, carry, k=k):
            for u in range(8):
                q = step * 8 + u
                tile = table[idx_ref[k, q]].astype(F32)
                turned = pltpu.roll(tile, 64, 1)
                out_ref[k, q, 0:16] = jnp.where(low, tile, turned).astype(BF16)
                out_ref[k, q, 16:32] = jnp.where(low, turned, tile).astype(BF16)
            return carry

        lax.fori_loop(0, 4, some, 0)


def pick(idx, parts):
    return pl.pallas_call(
        pick_kernel,
        in_specs=[pl.BlockSpec(memory_space=SMEM)] + [pl.BlockSpec(memory_space=pl.ANY)] * 10,
        out_specs=pl.BlockSpec(memory_space=VMEM),
        out_shape=jax.ShapeDtypeStruct((8, 32, 32, 128), BF16),
        scratch_shapes=[VMEM((2048, 16, 128), BF16), pltpu.SemaphoreType.DMA((10,))],
        cost_estimate=pl.CostEstimate(flops=1 << 21, bytes_accessed=10 << 20, transcendentals=0),
        name="pick",
    )(idx, *parts)


def q_kernel(par, phase_ref, a0, a1, a2, a3, o0, o1, o2, o3):
    arrays = (a0, a1, a2, a3)
    outs = (o0, o1, o2, o3)
    pieces = []
    for part in range(2):
        for zd in range(4):
            for xd in range(4):
                for cd in range(2):
                    if par == 0:
                        pieces.append(arrays[zd][xd * 2 + cd, part])
                    else:
                        pieces.append(arrays[xd][zd * 2 + cd, part])
    stacked = jnp.concatenate(pieces, 0)
    result = jnp.dot(phase_ref[...], stacked, preferred_element_type=F32).astype(BF16)
    for part in range(2):
        for bd in range(4):
            at = (part * 4 + bd) * 32
            outs[bd][part] = result[at : at + 32]


def q_transform(par, phase, arrays):
    return pl.pallas_call(
        functools.partial(q_kernel, par),
        grid=(4,),
        in_specs=[pl.BlockSpec((256, 1024), lambda k: (0, 0))]
        + [pl.BlockSpec((8, 2, None, 16, 256), lambda k: (0, 0, k, 0, 0))] * 4,
        out_specs=[pl.BlockSpec((None, 2, 32, 256), lambda k: (k, 0, 0, 0))] * 4,
        out_shape=[jax.ShapeDtypeStruct((4, 2, 32, 256), BF16)] * 4,
        cost_estimate=pl.CostEstimate(
            flops=2 * 4 * 256 * 1024 * 256, bytes_accessed=3 << 20, transcendentals=0
        ),
        name=f"q_transform_{par}",
    )(phase, *arrays)


def rotate_kernel(me_ref, eig_ref, w_ref, a0, a1, a2, a3, out_ref, halves, squares):
    b = me_ref[3]
    arrays = (a0, a1, a2, a3)
    left = jnp.concatenate([ref[0] for ref in arrays], 0)
    right = jnp.concatenate([ref[1] for ref in arrays], 0)
    both = jnp.concatenate([left, right], 1)
    eig_r = eig_ref[0:32]
    eig_i = eig_ref[32:64]

    def padded(block, il):
        blocks = []
        if il:
            blocks.append(jnp.zeros((il * 32, 256), BF16))
        blocks.append(block)
        if il < 7:
            blocks.append(jnp.zeros(((7 - il) * 32, 256), BF16))
        return jnp.concatenate(blocks, 0)

    for il in range(8):
        weights = jnp.concatenate([padded(eig_r, il), padded(eig_i, il)], 0)
        half = jnp.dot(both, weights, preferred_element_type=F32)
        for bd in range(4):
            at = pl.multiple_of(lax.rem(b + bd, 4) * 256 + il * 32, 32)
            halves[0, pl.ds(at, 32), :] = half[bd * 32 : bd * 32 + 32, 0:128]
            halves[1, pl.ds(at, 32), :] = half[bd * 32 : bd * 32 + 32, 128:256]

    lane = lax.broadcasted_iota(jnp.int32, (32, 128), 1)
    zeros = jnp.zeros((32, 128), BF16)
    keep_low = jnp.where(lane < 64, 1.0, 0.0).astype(BF16)
    keep_high = jnp.where(lane < 64, 0.0, 1.0).astype(BF16)
    for group in range(8):
        rows = []
        lhs = []
        for j in range(4):
            q = group * 4 + j
            rows.append(halves[0, pl.ds(q, 32, stride=32), :].astype(BF16))
            rows.append(halves[1, pl.ds(q, 32, stride=32), :].astype(BF16))
            kept = w_ref[q] * (keep_high if j % 2 else keep_low)
            lhs.append(jnp.concatenate([zeros, kept] if j >= 2 else [kept, zeros], 1))
        rotated = jnp.dot(
            jnp.concatenate(lhs, 0), jnp.concatenate(rows, 0), preferred_element_type=F32
        )
        square = rotated * rotated
        squares[group * 128 : group * 128 + 128, :] = square + pltpu.roll(square, 32, 1)

    quarter = lane // 32
    for g in range(8):
        parts = [squares[pl.ds(4 * g + mm, 32, stride=32), :] for mm in range(4)]
        merged = jnp.where(
            quarter == 0,
            parts[0],
            jnp.where(quarter == 1, parts[1], jnp.where(quarter == 2, parts[2], parts[3])),
        )
        out_ref[:, g * 128 : g * 128 + 128] = merged.astype(BF16)


def rotate(par, me, eig, picked, arrays):
    return pl.pallas_call(
        rotate_kernel,
        grid=(4,),
        in_specs=[
            pl.BlockSpec(memory_space=SMEM),
            pl.BlockSpec((None, 64, 256), lambda k: (2 * k + par, 0, 0)),
            pl.BlockSpec((None, 32, 32, 128), lambda k: (2 * k + par, 0, 0, 0)),
        ]
        + [pl.BlockSpec((None, 2, 32, 256), lambda k: (k, 0, 0, 0))] * 4,
        out_specs=pl.BlockSpec((None, 32, 1024), lambda k: (k, 0, 0)),
        out_shape=jax.ShapeDtypeStruct((4, 32, 1024), BF16),
        scratch_shapes=[VMEM((2, 1024, 128), F32), VMEM((1024, 128), F32)],
        cost_estimate=pl.CostEstimate(
            flops=2 * 4 * 8 * (128 * 512 * 256 + 128 * 256 * 128),
            bytes_accessed=3 << 20,
            transcendentals=0,
        ),
        name=f"rotate_{par}",
    )(me, eig, picked, *arrays)


def shards(g_wannier, k_angle, q_angle, eig_k, eig_kq, mask_k, mask_kq, owner, kq_local):
    row = lax.axis_index("row")
    b = lax.axis_index("blk")
    z, x, c = row // 8, (row // 2) % 4, row % 2
    me = jnp.stack([z, x, c, b]).astype(jnp.int32)

    table = table_of(eig_kq, mask_kq)
    along_x = jnp.stack([table] + [row_shift(table, dx=-d) for d in (1, 2, 3)])
    along_z = jnp.stack([along_x] + [row_shift(along_x, dz=-d) for d in (1, 2, 3)])
    y1 = blk_shift(along_z, -1)
    y3 = blk_shift(along_z, 1)
    y2a = blk_shift(y1[0:2], -1)
    y2b = blk_shift(y3[2:4], 1)
    own = [along_z, y1, y3, y2a, y2b]
    other = [row_shift(part, dc=1) for part in own]
    parts = [part.reshape(-1, 16, 128) for part in own + other]

    own_row = owner.reshape(8, 32) // 4
    c_off = (own_row - c) % 2
    y_off = (owner.reshape(8, 32) - b) % 4
    z_off = (own_row // 8 - z) % 4
    x_off = (own_row // 2 - x) % 4
    idx = (((c_off * 4 + y_off) * 4 + z_off) * 4 + x_off) * 16 + kq_local.reshape(8, 32)

    steps = np.arange(4)
    dc_all = np.arange(2)[None, :, None]
    x_first = row_id_of(
        z + steps[None, None, :], x + steps[:, None, None], c + dc_all
    ).reshape(32)
    z_first = row_id_of(
        z + steps[:, None, None], x + steps[None, None, :], c + dc_all
    ).reshape(32)
    gathered = []
    for par, dests in ((0, x_first), (1, z_first)):
        outs = k_transform(par, dests, k_angle, g_wannier)
        moved = {}
        for d in range(4):
            for dc in range(2):
                value = outs[d * 2 + dc]
                if d or dc:
                    value = row_shift(value, dc=dc, **{"dx" if par == 0 else "dz": d})
                moved[d, dc] = value
        final = {}
        for d in range(4):
            stacked = jnp.stack(
                [moved[(-off) % 4, dc][d] for off in range(4) for dc in range(2)]
            )
            if d:
                stacked = row_shift(stacked, **{"dz" if par == 0 else "dx": d})
            final[(-d) % 4] = stacked
        gathered.append([final[off] for off in range(4)])

    phase, eig = prep(me, q_angle, eig_k, mask_k)
    picked = pick(idx, parts)
    results = []
    for par in range(2):
        outs = q_transform(par, phase, gathered[par])
        arrays = {0: outs[0]}
        for d in (1, 2, 3):
            arrays[(-d) % 4] = blk_shift(outs[d], d)
        results.append(rotate(par, me, eig, picked, [arrays[off] for off in range(4)]))
    return jnp.transpose(jnp.stack(results, 1).reshape(8, 32, 1024), (1, 0, 2))


def row_id_of(z, x, c):
    return (((z % 4) * 4 + x % 4) * 2 + c % 2).astype(jnp.int32)


def solution(mesh):
    placed = (
        P("row", None, None, "blk"),
        P(),
        P(),
        P("row", None, None, None),
        P(("row", "blk"), None, None, None),
        P("row", None),
        P(("row", "blk"), None),
        P("blk", "row", None, None),
        P("blk", "row", None, None),
    )
    return jax.shard_map(
        shards, mesh=mesh, in_specs=placed, out_specs=P("blk", "row", None), check_vma=False
    )
```

```python
import jax
import jax.numpy as jnp
import numpy as np
from jax import lax
from jax.experimental import pallas as pl
from jax.experimental.pallas import tpu as pltpu
from jax.sharding import PartitionSpec as P


F32 = jnp.float32
BF16 = jnp.bfloat16
VMEM = pltpu.VMEM
SMEM = pltpu.SMEM


def fitted(fun, odd):
    top = 3.15**2
    nodes = 0.5 * top * (1 - np.cos(np.pi * (np.arange(64) + 0.5) / 64))
    root = np.sqrt(nodes)
    values = fun(root) / root if odd else fun(root)
    cheb = np.polynomial.chebyshev.Chebyshev.fit(nodes, values, 8, domain=[0, top])
    return [float(v) for v in cheb.convert(kind=np.polynomial.Polynomial).coef]


SIN_COEF = fitted(np.sin, True)
COS_COEF = fitted(np.cos, False)


def cos_sin(angle):
    square = angle * angle

    def horner(coef):
        total = jnp.full_like(square, coef[-1])
        for c in coef[-2::-1]:
            total = total * square + c
        return total

    return horner(COS_COEF), horner(SIN_COEF) * angle


def limit(mebibytes):
    return pltpu.CompilerParams(vmem_limit_bytes=mebibytes << 20)


def row_id(z, x, c):
    return ((z % 4) * 4 + x % 4) * 2 + c % 2


def row_shift(value, dz=0, dx=0, dc=0):
    pairs = [
        (row_id(z, x, c), row_id(z + dz, x + dx, c + dc))
        for z in range(4)
        for x in range(4)
        for c in range(2)
    ]
    return lax.ppermute(value, "row", pairs)


def blk_shift(value, dy):
    return lax.ppermute(value, "blk", [(y, (y + dy) % 4) for y in range(4)])


def k_phase_kernel(ang_ref, out_ref):
    cos, sin = cos_sin(ang_ref[...])
    cos = cos.astype(BF16)
    sin = sin.astype(BF16)
    out_ref[0:256, 0:512] = cos
    out_ref[0:256, 512:1024] = -sin
    out_ref[256:512, 0:512] = sin
    out_ref[256:512, 512:1024] = cos


def k_phase_of(k_angle):
    whole = pl.BlockSpec(memory_space=VMEM)
    return pl.pallas_call(
        k_phase_kernel,
        in_specs=[whole],
        out_specs=whole,
        out_shape=jax.ShapeDtypeStruct((512, 1024), BF16),
        cost_estimate=pl.CostEstimate(flops=1 << 23, bytes_accessed=2 << 20, transcendentals=0),
        compiler_params=limit(8),
        name="k_phase",
    )(k_angle)


def k_kernel(phase_ref, g_ref, out_ref, g_in, middle, packed, in_sems, out_sems):
    def load(rp):
        return pltpu.make_async_copy(g_ref.at[rp], g_in.at[rp], in_sems.at[rp])

    for rp in range(16):
        load(rp).start()

    def some(step, carry):
        for u in range(4):
            load(step * 4 + u).wait()
        for u in range(4):
            rp = step * 4 + u
            part = jnp.dot(
                phase_ref[...], g_in[rp].reshape(1024, 256), preferred_element_type=F32
            )
            middle[rp] = part.astype(BF16)
        return carry

    lax.fori_loop(0, 4, some, 0)

    def store(piece):
        at = pl.ds(piece * 4, 4)
        return pltpu.make_async_copy(packed.at[at], out_ref.at[at], out_sems.at[piece])

    for piece in range(8):
        for c in range(2):
            at = c * 256 + 32 * piece
            turned = jnp.swapaxes(middle[:, at : at + 32, :], 0, 1)
            packed[piece * 4 : piece * 4 + 4, c * 8 : c * 8 + 8] = turned.reshape(4, 8, 16, 256)
        store(piece).start()
    for piece in range(8):
        store(piece).wait()


def k_transform(phase, g):
    return pl.pallas_call(
        k_kernel,
        in_specs=[pl.BlockSpec(memory_space=VMEM), pl.BlockSpec(memory_space=pltpu.HBM)],
        out_specs=pl.BlockSpec(memory_space=pltpu.HBM),
        out_shape=jax.ShapeDtypeStruct((32, 16, 16, 256), BF16),
        scratch_shapes=[
            VMEM((16, 2, 512, 256), BF16),
            VMEM((16, 512, 256), BF16),
            VMEM((32, 16, 16, 256), BF16),
            pltpu.SemaphoreType.DMA((16,)),
            pltpu.SemaphoreType.DMA((8,)),
        ],
        cost_estimate=pl.CostEstimate(
            flops=2 * 16 * 512 * 1024 * 256, bytes_accessed=12 << 20, transcendentals=0
        ),
        compiler_params=limit(58),
        name="k_transform",
    )(phase, g)


def prep_kernel(me_ref, q_ref, eig_ref, mask_ref, phase_out, eig_out):
    b = me_ref[3]
    for bd in range(4):
        rows = pl.ds(pl.multiple_of(lax.rem(b + bd, 4) * 32, 32), 32)
        cos, sin = cos_sin(q_ref[rows, :])
        cos = cos.astype(BF16)
        sin = sin.astype(BF16)
        top = slice(bd * 32, bd * 32 + 32)
        low = slice(128 + bd * 32, 128 + bd * 32 + 32)
        phase_out[top, 0:512] = cos
        phase_out[top, 512:1024] = -sin
        phase_out[low, 0:512] = sin
        phase_out[low, 512:1024] = cos
    for k in range(8):
        mask = mask_ref[k : k + 1, :].astype(F32)
        er = eig_ref[k, 0].astype(F32) * mask
        ei = eig_ref[k, 1].astype(F32) * mask
        first = [er, ei, er, ei, ei, -er, ei, -er]
        second = [-ei, er, -ei, er, er, ei, er, ei]
        eig_out[k, 0:32] = jnp.concatenate(first, 1).astype(BF16)
        eig_out[k, 32:64] = jnp.concatenate(second, 1).astype(BF16)


def prep(me, q_angle, eig_k, mask_k):
    whole = pl.BlockSpec(memory_space=VMEM)
    return pl.pallas_call(
        prep_kernel,
        in_specs=[pl.BlockSpec(memory_space=SMEM), whole, whole, whole],
        out_specs=[whole, whole],
        out_shape=[
            jax.ShapeDtypeStruct((256, 1024), BF16),
            jax.ShapeDtypeStruct((8, 64, 256), BF16),
        ],
        cost_estimate=pl.CostEstimate(flops=1 << 22, bytes_accessed=1 << 20, transcendentals=0),
        compiler_params=limit(8),
        name="prep",
    )(me, q_angle, eig_k, mask_k)


def table_kernel(eig_ref, mask_ref, out_ref):
    for p in range(16):
        mask = mask_ref[p : p + 1, :].astype(F32)
        both = jnp.concatenate([eig_ref[p, 0], eig_ref[p, 1]], 0).astype(F32) * mask
        turned = jnp.transpose(both)
        out_ref[p] = jnp.concatenate([turned[0:16], turned[16:32]], 1).astype(BF16)


def table_of(eig_kq, mask_kq):
    whole = pl.BlockSpec(memory_space=VMEM)
    return pl.pallas_call(
        table_kernel,
        in_specs=[whole, whole],
        out_specs=whole,
        out_shape=jax.ShapeDtypeStruct((16, 16, 128), BF16),
        cost_estimate=pl.CostEstimate(flops=1 << 20, bytes_accessed=1 << 18, transcendentals=0),
        compiler_params=limit(8),
        name="table",
    )(eig_kq, mask_kq)


def pick_kernel(me_ref, idx_ref, *refs):
    parts, out_ref = refs[:10], refs[10]
    table, spread, sems = refs[11:]
    k = pl.program_id(0)

    @pl.when(k == 0)
    def _():
        copies = []
        for cd in range(2):
            own, y1, y3, y2a, y2b = parts[cd * 5 : cd * 5 + 5]
            at = cd * 1024
            for ref, start, size in (
                (own, at, 256),
                (y1, at + 256, 256),
                (y2a, at + 512, 128),
                (y2b, at + 640, 128),
                (y3, at + 768, 256),
            ):
                copies.append(
                    pltpu.make_async_copy(ref, table.at[pl.ds(start, size)], sems.at[len(copies)])
                )
        for copy in copies:
            copy.start()
        source = lax.broadcasted_iota(jnp.int32, (128, 1024), 0)
        target = lax.broadcasted_iota(jnp.int32, (128, 1024), 1) // 8
        wanted = (target // 32) * 32 + (target + 8 * me_ref[3]) % 32
        spread[...] = jnp.where(source == wanted, 1.0, 0.0).astype(BF16)
        for copy in copies:
            copy.wait()

    row = lax.broadcasted_iota(jnp.int32, (128, 512), 0)
    lane = lax.broadcasted_iota(jnp.int32, (128, 512), 1)
    same = row % 8 == lane % 8
    groups = []
    for group in range(4):
        tiles = jnp.stack([table[idx_ref[k, group * 8 + u]].astype(F32) for u in range(8)])
        groups.append(jnp.swapaxes(tiles, 0, 1).reshape(128, 128).astype(BF16))
    tiles = jnp.concatenate(groups, 0)
    for h in range(2):
        at = slice(h * 512, h * 512 + 512)
        wide = jnp.dot(tiles, spread[:, at], preferred_element_type=F32)
        for group in range(4):
            kept = jnp.where(same, wide[group * 128 : group * 128 + 128], 0.0)
            out_ref[group, h * 128 : h * 128 + 128] = kept.astype(BF16)


def pick(me, idx, parts):
    return pl.pallas_call(
        pick_kernel,
        grid=(8,),
        in_specs=[pl.BlockSpec(memory_space=SMEM)] * 2 + [pl.BlockSpec(memory_space=pl.ANY)] * 10,
        out_specs=pl.BlockSpec((None, 4, 256, 512), lambda k: (k, 0, 0, 0)),
        out_shape=jax.ShapeDtypeStruct((8, 4, 256, 512), BF16),
        scratch_shapes=[
            VMEM((2048, 16, 128), BF16),
            VMEM((128, 1024), BF16),
            pltpu.SemaphoreType.DMA((10,)),
        ],
        cost_estimate=pl.CostEstimate(
            flops=2 * 32 * 128 * 128 * 1024, bytes_accessed=18 << 20, transcendentals=0
        ),
        compiler_params=limit(16),
        name="pick",
    )(me, idx, *parts)


def q_kernel(phase_ref, data_ref, o0, o1, o2, o3, data, sems):
    outs = (o0, o1, o2, o3)

    def load(k, part):
        return pltpu.make_async_copy(
            data_ref.at[:, part * 8 + k], data.at[k, part], sems.at[k, part]
        )

    for k in range(8):
        for part in range(2):
            load(k, part).start()
    for first in (0, 4):
        for k in range(first, first + 4):
            for part in range(2):
                load(k, part).wait()
        for k in range(first, first + 4):
            stacked = data[k].reshape(1024, 256)
            result = jnp.dot(phase_ref[...], stacked, preferred_element_type=F32).astype(BF16)
            for part in range(2):
                for bd in range(4):
                    at = (part * 4 + bd) * 32
                    outs[bd][k, part] = result[at : at + 32]


def q_transform(phase, data):
    whole = pl.BlockSpec(memory_space=VMEM)
    return pl.pallas_call(
        q_kernel,
        in_specs=[whole, pl.BlockSpec(memory_space=pl.ANY)],
        out_specs=[whole] * 4,
        out_shape=[jax.ShapeDtypeStruct((8, 2, 32, 256), BF16)] * 4,
        scratch_shapes=[
            VMEM((8, 2, 32, 16, 256), BF16),
            pltpu.SemaphoreType.DMA((8, 2)),
        ],
        cost_estimate=pl.CostEstimate(
            flops=2 * 8 * 256 * 1024 * 256, bytes_accessed=6 << 20, transcendentals=0
        ),
        compiler_params=limit(12),
        name="q_transform",
    )(phase, data)


def rotate_kernel(eig_ref, w_ref, a0, a1, a2, a3, out_ref, even, odd, merged, done):
    arrays = (a0, a1, a2, a3)
    quarter = lax.broadcasted_iota(jnp.int32, (8, 128), 1) // 32

    def first(k, halves):
        columns = []
        for part in range(2):
            whole = jnp.concatenate([ref[k, part] for ref in arrays], 0)
            columns.append((whole[:, 0:128], whole[:, 128:256]))
        both = jnp.concatenate(
            [jnp.concatenate([columns[0][hi], columns[1][hi]], 1) for hi in range(2)], 0
        )
        for low in range(4):
            blocks = []
            for part in range(2):
                for at in range(4):
                    block = eig_ref[k, part * 32 : part * 32 + 32]
                    blocks.append(block if at == low else jnp.zeros_like(block))
            half = jnp.dot(both, jnp.concatenate(blocks, 0), preferred_element_type=F32)
            for hi in range(2):
                for bd in range(4):
                    for group in range(4):
                        at = hi * 128 + bd * 32 + group * 8
                        place = (bd * 8 + hi * 4 + low) * 8
                        halves[group, place : place + 8] = half[at : at + 8, 0:128]
                        halves[group, 256 + place : 264 + place] = half[at : at + 8, 128:256]

    def second(k, halves):
        for group in range(4):
            rotated = jnp.dot(
                w_ref[k, group], halves[group].astype(BF16), preferred_element_type=F32
            )
            square = rotated * rotated
            square = square + pltpu.roll(square, 32, 1)
            for m in range(8):
                parts = [square[(4 * m + mm) * 8 : (4 * m + mm) * 8 + 8] for mm in range(4)]
                merged[group * 8 : group * 8 + 8, m * 128 : m * 128 + 128] = jnp.where(
                    quarter == 0,
                    parts[0],
                    jnp.where(
                        quarter == 1, parts[1], jnp.where(quarter == 2, parts[2], parts[3])
                    ),
                )
        done[k] = merged[...].astype(BF16)

    first(0, even)

    def two(step, carry):
        first(2 * step + 1, odd)
        second(2 * step, even)
        first(2 * step + 2, even)
        second(2 * step + 1, odd)
        return carry

    lax.fori_loop(0, 3, two, 0)
    first(7, odd)
    second(6, even)
    second(7, odd)
    out_ref[...] = jnp.swapaxes(done[...], 0, 1)


def rotate(eig, picked, arrays):
    whole = pl.BlockSpec(memory_space=VMEM)
    return pl.pallas_call(
        rotate_kernel,
        in_specs=[whole] * 6,
        out_specs=whole,
        out_shape=jax.ShapeDtypeStruct((32, 8, 1024), BF16),
        scratch_shapes=[
            VMEM((4, 512, 128), F32),
            VMEM((4, 512, 128), F32),
            VMEM((32, 1024), F32),
            VMEM((8, 32, 1024), BF16),
        ],
        cost_estimate=pl.CostEstimate(
            flops=2 * 8 * 4 * (256 * 256 * 256 + 256 * 512 * 128),
            bytes_accessed=12 << 20,
            transcendentals=0,
        ),
        compiler_params=limit(12),
        name="rotate",
    )(eig, picked, *arrays)


def shards(g_wannier, k_angle, q_angle, eig_k, eig_kq, mask_k, mask_kq, owner, kq_local):
    row = lax.axis_index("row")
    b = lax.axis_index("blk")
    z, x, c = row // 8, (row // 2) % 4, row % 2
    me = jnp.stack([z, x, c, b]).astype(jnp.int32)

    table = table_of(eig_kq, mask_kq)
    table, k_angle = lax.optimization_barrier((table, k_angle))
    from_x = []
    for d in (1, 2, 3):
        from_x.append(row_shift(table, dx=-d))
    along_x = jnp.stack([table] + from_x)
    from_z = []
    for d in (1, 2, 3):
        from_z.append(row_shift(along_x, dz=-d))
    along_z = jnp.stack([along_x] + from_z)
    y1 = blk_shift(along_z, -1)
    y3 = blk_shift(along_z, 1)
    y2a = blk_shift(y1[0:2], -1)
    y2b = blk_shift(y3[2:4], 1)
    own = [along_z, y1, y3, y2a, y2b]
    other = [row_shift(part, dc=1) for part in own]
    parts = [part.reshape(-1, 16, 128) for part in own + other]

    own_row = owner.reshape(8, 32) // 4
    c_off = (own_row - c) % 2
    y_off = (owner.reshape(8, 32) - b) % 4
    z_off = (own_row // 8 - z) % 4
    x_off = (own_row // 2 - x) % 4
    idx = (((c_off * 4 + y_off) * 4 + z_off) * 4 + x_off) * 16 + kq_local.reshape(8, 32)

    k_phase = k_phase_of(k_angle)
    sent = k_transform(k_phase, g_wannier)
    taken = lax.all_to_all(sent, "row", split_axis=0, concat_axis=0, tiled=True)

    phase, eig = prep(me, q_angle, eig_k, mask_k)
    picked = pick(me, idx, parts)
    outs = q_transform(phase, taken)
    arrays = {0: outs[0]}
    for d in (1, 2, 3):
        arrays[(-d) % 4] = blk_shift(outs[d], d)
    return rotate(eig, picked, [arrays[off] for off in range(4)])


def solution(mesh):
    placed = (
        P("row", None, None, "blk"),
        P(),
        P(),
        P("row", None, None, None),
        P(("row", "blk"), None, None, None),
        P("row", None),
        P(("row", "blk"), None),
        P("blk", "row", None, None),
        P("blk", "row", None, None),
    )

    return jax.shard_map(
        shards, mesh=mesh, in_specs=placed, out_specs=P("blk", "row", None), check_vma=False
    )
```

```python
import functools

import jax
import jax.numpy as jnp
import numpy as np
from jax import lax
from jax.experimental import pallas as pl
from jax.experimental.pallas import tpu as pltpu
from jax.sharding import PartitionSpec as P


SPLIT = (4, 4)

F32 = jnp.float32
BF16 = jnp.bfloat16
VMEM = pltpu.VMEM
SMEM = pltpu.SMEM


def fitted(fun, odd):
    top = 3.15**2
    nodes = 0.5 * top * (1 - np.cos(np.pi * (np.arange(64) + 0.5) / 64))
    root = np.sqrt(nodes)
    values = fun(root) / root if odd else fun(root)
    cheb = np.polynomial.chebyshev.Chebyshev.fit(nodes, values, 8, domain=[0, top])
    return [float(v) for v in cheb.convert(kind=np.polynomial.Polynomial).coef]


SIN_COEF = fitted(np.sin, True)
COS_COEF = fitted(np.cos, False)


def cos_sin(angle):
    square = angle * angle

    def horner(coef):
        total = jnp.full_like(square, coef[-1])
        for c in coef[-2::-1]:
            total = total * square + c
        return total

    return horner(COS_COEF), horner(SIN_COEF) * angle


def limit(mebibytes):
    return pltpu.CompilerParams(vmem_limit_bytes=mebibytes << 20)


def row_id(z, x, c):
    return ((z % 4) * 4 + x % 4) * 2 + c % 2


def row_shift(value, dz=0, dx=0, dc=0):
    pairs = [
        (row_id(z, x, c), row_id(z + dz, x + dx, c + dc))
        for z in range(4)
        for x in range(4)
        for c in range(2)
    ]
    return lax.ppermute(value, "row", pairs)


def blk_shift(value, dy):
    return lax.ppermute(value, "blk", [(y, (y + dy) % 4) for y in range(4)])


def k_phase_kernel(ang_ref, out_ref):
    cos, sin = cos_sin(ang_ref[...])
    cos = jnp.swapaxes(cos.reshape(32, 8, 512), 0, 1).astype(BF16)
    sin = jnp.swapaxes(sin.reshape(32, 8, 512), 0, 1).astype(BF16)
    out_ref[:, 0, :, 0:512] = cos
    out_ref[:, 0, :, 512:1024] = -sin
    out_ref[:, 1, :, 0:512] = sin
    out_ref[:, 1, :, 512:1024] = cos


def k_phase_of(k_angle):
    whole = pl.BlockSpec(memory_space=VMEM)
    return pl.pallas_call(
        k_phase_kernel,
        in_specs=[whole],
        out_specs=whole,
        out_shape=jax.ShapeDtypeStruct((8, 2, 32, 1024), BF16),
        cost_estimate=pl.CostEstimate(flops=1 << 23, bytes_accessed=2 << 20, transcendentals=0),
        compiler_params=limit(8),
        name="k_phase",
    )(k_angle)


def k_kernel(start, count, phase_ref, g_ref, out_ref, g_in, middle, packed, in_sems, out_sems):
    def load(rp):
        return pltpu.make_async_copy(g_ref.at[rp], g_in.at[rp], in_sems.at[rp])

    for rp in range(16):
        load(rp).start()

    def some(step, carry):
        for u in range(4):
            load(step * 4 + u).wait()
        for u in range(4):
            rp = step * 4 + u
            phase = phase_ref[start : start + count].reshape(count * 64, 1024)
            part = jnp.dot(phase, g_in[rp].reshape(1024, 256), preferred_element_type=F32)
            middle[rp] = part.astype(BF16)
        return carry

    lax.fori_loop(0, 4, some, 0)

    def store(at):
        return pltpu.make_async_copy(packed.at[:, at], out_ref.at[:, at], out_sems.at[at])

    for at in range(2 * count):
        packed[:, at] = jnp.swapaxes(middle[:, at * 32 : at * 32 + 32, :], 0, 1)
        store(at).start()
    for at in range(2 * count):
        store(at).wait()


def k_transform(start, count, phase, g):
    return pl.pallas_call(
        functools.partial(k_kernel, start, count),
        in_specs=[pl.BlockSpec(memory_space=VMEM), pl.BlockSpec(memory_space=pl.ANY)],
        out_specs=pl.BlockSpec(memory_space=pl.ANY),
        out_shape=jax.ShapeDtypeStruct((32, 2 * count, 16, 256), BF16),
        scratch_shapes=[
            VMEM((16, 2, 512, 256), BF16),
            VMEM((16, 64 * count, 256), BF16),
            VMEM((32, 2 * count, 16, 256), BF16),
            pltpu.SemaphoreType.DMA((16,)),
            pltpu.SemaphoreType.DMA((2 * count,)),
        ],
        cost_estimate=pl.CostEstimate(
            flops=2 * 16 * 64 * count * 1024 * 256, bytes_accessed=10 << 20, transcendentals=0
        ),
        compiler_params=limit(56),
    )(phase, g)


def prep_kernel(me_ref, q_ref, eig_ref, mask_ref, phase_out, eig_out):
    b = me_ref[3]
    for bd in range(4):
        rows = pl.ds(pl.multiple_of(lax.rem(b + bd, 4) * 32, 32), 32)
        cos, sin = cos_sin(q_ref[rows, :])
        cos = cos.astype(BF16)
        sin = sin.astype(BF16)
        top = slice(bd * 32, bd * 32 + 32)
        low = slice(128 + bd * 32, 128 + bd * 32 + 32)
        phase_out[top, 0:512] = cos
        phase_out[top, 512:1024] = -sin
        phase_out[low, 0:512] = sin
        phase_out[low, 512:1024] = cos
    for k in range(8):
        mask = mask_ref[k : k + 1, :].astype(F32)
        er = eig_ref[k, 0].astype(F32) * mask
        ei = eig_ref[k, 1].astype(F32) * mask
        first = [er, ei, er, ei, ei, -er, ei, -er]
        second = [-ei, er, -ei, er, er, ei, er, ei]
        eig_out[k, 0:32] = jnp.concatenate(first, 1).astype(BF16)
        eig_out[k, 32:64] = jnp.concatenate(second, 1).astype(BF16)


def prep(me, q_angle, eig_k, mask_k):
    whole = pl.BlockSpec(memory_space=VMEM)
    return pl.pallas_call(
        prep_kernel,
        in_specs=[pl.BlockSpec(memory_space=SMEM), whole, whole, whole],
        out_specs=[whole, whole],
        out_shape=[
            jax.ShapeDtypeStruct((256, 1024), BF16),
            jax.ShapeDtypeStruct((8, 64, 256), BF16),
        ],
        cost_estimate=pl.CostEstimate(flops=1 << 22, bytes_accessed=1 << 20, transcendentals=0),
        compiler_params=limit(8),
        name="prep",
    )(me, q_angle, eig_k, mask_k)


def table_kernel(eig_ref, mask_ref, out_ref):
    for p in range(16):
        mask = mask_ref[p : p + 1, :].astype(F32)
        both = jnp.concatenate([eig_ref[p, 0], eig_ref[p, 1]], 0).astype(F32) * mask
        turned = jnp.transpose(both)
        out_ref[p] = jnp.concatenate([turned[0:16], turned[16:32]], 1).astype(BF16)


def table_of(eig_kq, mask_kq):
    whole = pl.BlockSpec(memory_space=VMEM)
    return pl.pallas_call(
        table_kernel,
        in_specs=[whole, whole],
        out_specs=whole,
        out_shape=jax.ShapeDtypeStruct((16, 16, 128), BF16),
        cost_estimate=pl.CostEstimate(flops=1 << 20, bytes_accessed=1 << 18, transcendentals=0),
        compiler_params=limit(8),
        name="table",
    )(eig_kq, mask_kq)


def pick_kernel(me_ref, idx_ref, *refs):
    parts, outs = refs[:16], refs[16:18]
    table, spread, blocks, sems, out_sems = refs[18:]
    k = pl.program_id(0)
    slot = lax.rem(k, 2)

    def store(out, at, place):
        return pltpu.make_async_copy(blocks.at[place], out.at[at], out_sems.at[place])

    @pl.when(k == 0)
    def _():
        copies = [
            pltpu.make_async_copy(part, table.at[pl.ds(at * 128, 128)], sems.at[at])
            for at, part in enumerate(parts)
        ]
        for copy in copies:
            copy.start()
        source = lax.broadcasted_iota(jnp.int32, (128, 1024), 0)
        target = lax.broadcasted_iota(jnp.int32, (128, 1024), 1) // 8
        wanted = (target // 32) * 32 + (target + 8 * me_ref[3]) % 32
        spread[...] = jnp.where(source == wanted, 1.0, 0.0).astype(BF16)
        for copy in copies:
            copy.wait()

    row = lax.broadcasted_iota(jnp.int32, (128, 512), 0)
    lane = lax.broadcasted_iota(jnp.int32, (128, 512), 1)
    same = row % 8 == lane % 8
    groups = []
    for group in range(4):
        tiles = jnp.stack([table[idx_ref[k, group * 8 + u]].astype(F32) for u in range(8)])
        groups.append(jnp.swapaxes(tiles, 0, 1).reshape(128, 128).astype(BF16))
    tiles = jnp.concatenate(groups, 0)

    @pl.when(k >= 2)
    def _():
        store(outs[0], 0, slot).wait()

    for h in range(2):
        at = slice(h * 512, h * 512 + 512)
        wide = jnp.dot(tiles, spread[:, at], preferred_element_type=F32)
        for group in range(4):
            kept = jnp.where(same, wide[group * 128 : group * 128 + 128], 0.0)
            blocks[slot, group, h * 128 : h * 128 + 128] = kept.astype(BF16)

    @pl.when(k < SPLIT[0])
    def _():
        store(outs[0], k, slot).start()

    @pl.when(k >= SPLIT[0])
    def _():
        store(outs[1], k - SPLIT[0], slot).start()

    @pl.when(k == 7)
    def _():
        store(outs[1], 0, 0).wait()
        store(outs[1], 0, 1).wait()


def pick(me, idx, parts):
    return pl.pallas_call(
        pick_kernel,
        grid=(8,),
        in_specs=[pl.BlockSpec(memory_space=SMEM)] * 2 + [pl.BlockSpec(memory_space=pl.ANY)] * 16,
        out_specs=[pl.BlockSpec(memory_space=pl.ANY)] * 2,
        out_shape=[jax.ShapeDtypeStruct((count, 4, 256, 512), BF16) for count in SPLIT],
        scratch_shapes=[
            VMEM((2048, 16, 128), BF16),
            VMEM((128, 1024), BF16),
            VMEM((2, 4, 256, 512), BF16),
            pltpu.SemaphoreType.DMA((16,)),
            pltpu.SemaphoreType.DMA((2,)),
        ],
        cost_estimate=pl.CostEstimate(
            flops=2 * 32 * 128 * 128 * 1024, bytes_accessed=18 << 20, transcendentals=0
        ),
        compiler_params=limit(16),
        name="pick",
    )(me, idx, *parts)


def q_kernel(start, count, phase_ref, data_ref, o0, o1, o2, o3, data, phase, sems, phase_sem):
    outs = (o0, o1, o2, o3)
    load_phase = pltpu.make_async_copy(phase_ref, phase, phase_sem)
    load_phase.start()

    def load(k, part):
        return pltpu.make_async_copy(
            data_ref.at[:, 2 * (start + k) + part], data.at[k, part], sems.at[k, part]
        )

    for k in range(count):
        for part in range(2):
            load(k, part).start()
    load_phase.wait()
    for k in range(count):
        for part in range(2):
            load(k, part).wait()
    for k in range(count):
        stacked = data[k].reshape(1024, 256)
        result = jnp.dot(phase[...], stacked, preferred_element_type=F32).astype(BF16)
        for part in range(2):
            for bd in range(4):
                at = (part * 4 + bd) * 32
                outs[bd][k, part] = result[at : at + 32]


def q_transform(start, count, phase, data):
    whole = pl.BlockSpec(memory_space=VMEM)
    return pl.pallas_call(
        functools.partial(q_kernel, start, count),
        in_specs=[pl.BlockSpec(memory_space=pl.ANY)] * 2,
        out_specs=[whole] * 4,
        out_shape=[jax.ShapeDtypeStruct((count, 2, 32, 256), BF16)] * 4,
        scratch_shapes=[
            VMEM((count, 2, 32, 16, 256), BF16),
            VMEM((256, 1024), BF16),
            pltpu.SemaphoreType.DMA((count, 2)),
            pltpu.SemaphoreType.DMA,
        ],
        cost_estimate=pl.CostEstimate(
            flops=2 * count * 256 * 1024 * 256, bytes_accessed=3 << 20, transcendentals=0
        ),
        compiler_params=limit(12),
    )(phase, data)


def rotate_kernel(start, count, eig_ref, w_ref, a0, a1, a2, a3, *refs):
    before = refs[0] if start else None
    out_ref, even, odd, merged, done = refs[1 if start else 0 :]
    arrays = (a0, a1, a2, a3)
    quarter = lax.broadcasted_iota(jnp.int32, (8, 128), 1) // 32

    def first(k, halves):
        columns = []
        for part in range(2):
            whole = jnp.concatenate([ref[k, part] for ref in arrays], 0)
            columns.append((whole[:, 0:128], whole[:, 128:256]))
        both = jnp.concatenate(
            [jnp.concatenate([columns[0][hi], columns[1][hi]], 1) for hi in range(2)], 0
        )
        for low in range(4):
            blocks = []
            for part in range(2):
                for at in range(4):
                    block = eig_ref[k + start, part * 32 : part * 32 + 32]
                    blocks.append(block if at == low else jnp.zeros_like(block))
            half = jnp.dot(both, jnp.concatenate(blocks, 0), preferred_element_type=F32)
            for hi in range(2):
                for bd in range(4):
                    for group in range(4):
                        at = hi * 128 + bd * 32 + group * 8
                        place = (bd * 8 + hi * 4 + low) * 8
                        halves[group, place : place + 8] = half[at : at + 8, 0:128]
                        halves[group, 256 + place : 264 + place] = half[at : at + 8, 128:256]

    def second(k, halves):
        for group in range(4):
            rotated = jnp.dot(
                w_ref[k, group], halves[group].astype(BF16), preferred_element_type=F32
            )
            square = rotated * rotated
            square = square + pltpu.roll(square, 32, 1)
            for m in range(8):
                parts = [square[(4 * m + mm) * 8 : (4 * m + mm) * 8 + 8] for mm in range(4)]
                merged[group * 8 : group * 8 + 8, m * 128 : m * 128 + 128] = jnp.where(
                    quarter == 0,
                    parts[0],
                    jnp.where(
                        quarter == 1, parts[1], jnp.where(quarter == 2, parts[2], parts[3])
                    ),
                )
        done[k] = merged[...].astype(BF16)

    slots = (even, odd)
    first(0, even)
    for k in range(count):
        if k + 1 < count:
            first(k + 1, slots[(k + 1) % 2])
        second(k, slots[k % 2])
    if start:
        out_ref[...] = jnp.swapaxes(jnp.concatenate([before[...], done[...]], 0), 0, 1)
    else:
        out_ref[...] = done[...]


def rotate(start, count, eig, picked, arrays, before=None):
    whole = pl.BlockSpec(memory_space=VMEM)
    out = (32, 8, 1024) if start else (count, 32, 1024)
    return pl.pallas_call(
        functools.partial(rotate_kernel, start, count),
        in_specs=[whole] * (7 if start else 6),
        out_specs=whole,
        out_shape=jax.ShapeDtypeStruct(out, BF16),
        scratch_shapes=[
            VMEM((4, 512, 128), F32),
            VMEM((4, 512, 128), F32),
            VMEM((32, 1024), F32),
            VMEM((count, 32, 1024), BF16),
        ],
        cost_estimate=pl.CostEstimate(
            flops=2 * count * 4 * (256 * 256 * 256 + 256 * 512 * 128),
            bytes_accessed=6 << 20,
            transcendentals=0,
        ),
        compiler_params=limit(10),
    )(eig, picked, *arrays, *([before] if start else []))


def shards(g_wannier, k_angle, q_angle, eig_k, eig_kq, mask_k, mask_kq, owner, kq_local):
    row = lax.axis_index("row")
    b = lax.axis_index("blk")
    z, x, c = row // 8, (row // 2) % 4, row % 2
    me = jnp.stack([z, x, c, b]).astype(jnp.int32)

    table = table_of(eig_kq, mask_kq)
    table, k_angle = lax.optimization_barrier((table, k_angle))
    from_x = []
    for d in (1, 2, 3):
        from_x.append(row_shift(table, dx=-d))
    along_x = jnp.stack([table] + from_x)
    from_z = []
    for d in (1, 2, 3):
        from_z.append(row_shift(along_x, dz=-d))
    halves = (jnp.stack([along_x, from_z[0]]), jnp.stack(from_z[1:]))
    own = {(0, 0): halves[0], (0, 1): halves[1]}
    for y, half, dy in ((1, 0, -1), (3, 1, 1), (1, 1, -1), (3, 0, 1)):
        own[y, half] = blk_shift(halves[half], dy)
    own[2, 0] = blk_shift(own[1, 0], -1)
    own[2, 1] = blk_shift(own[3, 1], 1)
    order = [(y, half) for y in range(4) for half in range(2)]
    parts = [own[at] for at in order]
    for y, half in order:
        parts.append(row_shift(own[y, half], dc=1))
    parts = [part.reshape(-1, 16, 128) for part in parts]

    own_row = owner.reshape(8, 32) // 4
    c_off = (own_row - c) % 2
    y_off = (owner.reshape(8, 32) - b) % 4
    z_off = (own_row // 8 - z) % 4
    x_off = (own_row // 2 - x) % 4
    idx = (((c_off * 4 + y_off) * 4 + z_off) * 4 + x_off) * 16 + kq_local.reshape(8, 32)

    k_phase = k_phase_of(k_angle)
    sent = k_transform(0, 8, k_phase, g_wannier)
    taken = lax.all_to_all(sent, "row", split_axis=0, concat_axis=0, tiled=True)

    phase, eig = prep(me, q_angle, eig_k, mask_k)
    picked = pick(me, idx, parts)
    result = None
    for par in range(2):
        outs = q_transform(par * SPLIT[0], SPLIT[par], phase, taken)
        arrays = {0: outs[0]}
        for d in (1, 2, 3):
            arrays[(-d) % 4] = blk_shift(outs[d], d)
        order = [arrays[off] for off in range(4)]
        result = rotate(par * SPLIT[0], SPLIT[par], eig, picked[par], order, result)
    return result


def solution(mesh):
    placed = (
        P("row", None, None, "blk"),
        P(),
        P(),
        P("row", None, None, None),
        P(("row", "blk"), None, None, None),
        P("row", None),
        P(("row", "blk"), None),
        P("blk", "row", None, None),
        P("blk", "row", None, None),
    )

    return jax.shard_map(
        shards, mesh=mesh, in_specs=placed, out_specs=P("blk", "row", None), check_vma=False
    )
```

```python
import functools

import jax
import jax.numpy as jnp
import numpy as np
from jax import lax
from jax.experimental import pallas as pl
from jax.experimental.pallas import tpu as pltpu
from jax.sharding import PartitionSpec as P


SPLIT = (4, 4)

F32 = jnp.float32
BF16 = jnp.bfloat16
VMEM = pltpu.VMEM
SMEM = pltpu.SMEM


def fitted(fun, odd):
    top = 3.15**2
    nodes = 0.5 * top * (1 - np.cos(np.pi * (np.arange(64) + 0.5) / 64))
    root = np.sqrt(nodes)
    values = fun(root) / root if odd else fun(root)
    cheb = np.polynomial.chebyshev.Chebyshev.fit(nodes, values, 8, domain=[0, top])
    return [float(v) for v in cheb.convert(kind=np.polynomial.Polynomial).coef]


SIN_COEF = fitted(np.sin, True)
COS_COEF = fitted(np.cos, False)


def cos_sin(angle):
    square = angle * angle

    def horner(coef):
        total = jnp.full_like(square, coef[-1])
        for c in coef[-2::-1]:
            total = total * square + c
        return total

    return horner(COS_COEF), horner(SIN_COEF) * angle


def limit(mebibytes):
    return pltpu.CompilerParams(vmem_limit_bytes=mebibytes << 20)


def row_id(z, x, c):
    return ((z % 4) * 4 + x % 4) * 2 + c % 2


def row_shift(value, dz=0, dx=0, dc=0):
    pairs = [
        (row_id(z, x, c), row_id(z + dz, x + dx, c + dc))
        for z in range(4)
        for x in range(4)
        for c in range(2)
    ]
    return lax.ppermute(value, "row", pairs)


def blk_shift(value, dy):
    return lax.ppermute(value, "blk", [(y, (y + dy) % 4) for y in range(4)])


def k_phase_kernel(ang_ref, out_ref):
    cos, sin = cos_sin(ang_ref[...])
    cos = jnp.swapaxes(cos.reshape(32, 8, 512), 0, 1).astype(BF16)
    sin = jnp.swapaxes(sin.reshape(32, 8, 512), 0, 1).astype(BF16)
    out_ref[:, 0, :, 0:512] = cos
    out_ref[:, 0, :, 512:1024] = -sin
    out_ref[:, 1, :, 0:512] = sin
    out_ref[:, 1, :, 512:1024] = cos


def k_phase_of(k_angle):
    whole = pl.BlockSpec(memory_space=VMEM)
    return pl.pallas_call(
        k_phase_kernel,
        in_specs=[whole],
        out_specs=whole,
        out_shape=jax.ShapeDtypeStruct((8, 2, 32, 1024), BF16),
        cost_estimate=pl.CostEstimate(flops=1 << 23, bytes_accessed=2 << 20, transcendentals=0),
        compiler_params=limit(8),
        name="k_phase",
    )(k_angle)


def k_kernel(start, count, phase_ref, g_ref, out_ref, g_in, middle, packed, in_sems, out_sems):
    def load(rp):
        return pltpu.make_async_copy(g_ref.at[rp], g_in.at[rp], in_sems.at[rp])

    for rp in range(16):
        load(rp).start()

    def some(step, carry):
        for u in range(4):
            load(step * 4 + u).wait()
        for u in range(4):
            rp = step * 4 + u
            phase = phase_ref[start : start + count].reshape(count * 64, 1024)
            part = jnp.dot(phase, g_in[rp].reshape(1024, 256), preferred_element_type=F32)
            middle[rp] = part.astype(BF16)
        return carry

    lax.fori_loop(0, 4, some, 0)

    def store(at):
        return pltpu.make_async_copy(packed.at[:, at], out_ref.at[:, at], out_sems.at[at])

    for at in range(2 * count):
        packed[:, at] = jnp.swapaxes(middle[:, at * 32 : at * 32 + 32, :], 0, 1)
        store(at).start()
    for at in range(2 * count):
        store(at).wait()


def k_transform(start, count, phase, g):
    return pl.pallas_call(
        functools.partial(k_kernel, start, count),
        in_specs=[pl.BlockSpec(memory_space=VMEM), pl.BlockSpec(memory_space=pl.ANY)],
        out_specs=pl.BlockSpec(memory_space=pl.ANY),
        out_shape=jax.ShapeDtypeStruct((32, 2 * count, 16, 256), BF16),
        scratch_shapes=[
            VMEM((16, 2, 512, 256), BF16),
            VMEM((16, 64 * count, 256), BF16),
            VMEM((32, 2 * count, 16, 256), BF16),
            pltpu.SemaphoreType.DMA((16,)),
            pltpu.SemaphoreType.DMA((2 * count,)),
        ],
        cost_estimate=pl.CostEstimate(
            flops=2 * 16 * 64 * count * 1024 * 256, bytes_accessed=10 << 20, transcendentals=0
        ),
        compiler_params=limit(56),
    )(phase, g)


def prep_kernel(me_ref, q_ref, eig_ref, mask_ref, phase_out, eig_out):
    b = me_ref[3]
    for bd in range(4):
        rows = pl.ds(pl.multiple_of(lax.rem(b + bd, 4) * 32, 32), 32)
        cos, sin = cos_sin(q_ref[rows, :])
        cos = cos.astype(BF16)
        sin = sin.astype(BF16)
        top = slice(bd * 32, bd * 32 + 32)
        low = slice(128 + bd * 32, 128 + bd * 32 + 32)
        phase_out[top, 0:512] = cos
        phase_out[top, 512:1024] = -sin
        phase_out[low, 0:512] = sin
        phase_out[low, 512:1024] = cos
    for k in range(8):
        mask = mask_ref[k : k + 1, :].astype(F32)
        er = eig_ref[k, 0].astype(F32) * mask
        ei = eig_ref[k, 1].astype(F32) * mask
        first = [er, ei, er, ei, ei, -er, ei, -er]
        second = [-ei, er, -ei, er, er, ei, er, ei]
        eig_out[k, 0:32] = jnp.concatenate(first, 1).astype(BF16)
        eig_out[k, 32:64] = jnp.concatenate(second, 1).astype(BF16)


def prep(me, q_angle, eig_k, mask_k):
    whole = pl.BlockSpec(memory_space=VMEM)
    return pl.pallas_call(
        prep_kernel,
        in_specs=[pl.BlockSpec(memory_space=SMEM), whole, whole, whole],
        out_specs=[whole, whole],
        out_shape=[
            jax.ShapeDtypeStruct((256, 1024), BF16),
            jax.ShapeDtypeStruct((8, 64, 256), BF16),
        ],
        cost_estimate=pl.CostEstimate(flops=1 << 22, bytes_accessed=1 << 20, transcendentals=0),
        compiler_params=limit(8),
        name="prep",
    )(me, q_angle, eig_k, mask_k)


def table_kernel(eig_ref, mask_ref, out_ref):
    for p in range(16):
        mask = mask_ref[p : p + 1, :].astype(F32)
        both = jnp.concatenate([eig_ref[p, 0], eig_ref[p, 1]], 0).astype(F32) * mask
        turned = jnp.transpose(both)
        out_ref[p] = jnp.concatenate([turned[0:16], turned[16:32]], 1).astype(BF16)


def table_of(eig_kq, mask_kq):
    whole = pl.BlockSpec(memory_space=VMEM)
    return pl.pallas_call(
        table_kernel,
        in_specs=[whole, whole],
        out_specs=whole,
        out_shape=jax.ShapeDtypeStruct((16, 16, 128), BF16),
        cost_estimate=pl.CostEstimate(flops=1 << 20, bytes_accessed=1 << 18, transcendentals=0),
        compiler_params=limit(8),
        name="table",
    )(eig_kq, mask_kq)


def pick_kernel(me_ref, idx_ref, *refs):
    parts, outs = refs[:16], refs[16:18]
    table, spread, blocks, sems, out_sems = refs[18:]
    k = pl.program_id(0)
    slot = lax.rem(k, 2)

    def store(out, at, place):
        return pltpu.make_async_copy(blocks.at[place], out.at[at], out_sems.at[place])

    @pl.when(k == 0)
    def _():
        copies = [
            pltpu.make_async_copy(part, table.at[pl.ds(at * 128, 128)], sems.at[at])
            for at, part in enumerate(parts)
        ]
        for copy in copies:
            copy.start()
        source = lax.broadcasted_iota(jnp.int32, (128, 1024), 0)
        target = lax.broadcasted_iota(jnp.int32, (128, 1024), 1) // 8
        wanted = (target // 32) * 32 + (target + 8 * me_ref[3]) % 32
        spread[...] = jnp.where(source == wanted, 1.0, 0.0).astype(BF16)
        for copy in copies:
            copy.wait()

    row = lax.broadcasted_iota(jnp.int32, (128, 512), 0)
    lane = lax.broadcasted_iota(jnp.int32, (128, 512), 1)
    same = row % 8 == lane % 8
    groups = []
    for group in range(4):
        tiles = jnp.stack([table[idx_ref[k, group * 8 + u]].astype(F32) for u in range(8)])
        groups.append(jnp.swapaxes(tiles, 0, 1).reshape(128, 128).astype(BF16))
    tiles = jnp.concatenate(groups, 0)

    @pl.when(k >= 2)
    def _():
        store(outs[0], 0, slot).wait()

    for h in range(2):
        at = slice(h * 512, h * 512 + 512)
        wide = jnp.dot(tiles, spread[:, at], preferred_element_type=F32)
        for group in range(4):
            kept = jnp.where(same, wide[group * 128 : group * 128 + 128], 0.0)
            blocks[slot, group, h * 128 : h * 128 + 128] = kept.astype(BF16)

    @pl.when(k < SPLIT[0])
    def _():
        store(outs[0], k, slot).start()

    @pl.when(k >= SPLIT[0])
    def _():
        store(outs[1], k - SPLIT[0], slot).start()

    @pl.when(k == 7)
    def _():
        store(outs[1], 0, 0).wait()
        store(outs[1], 0, 1).wait()


def pick(me, idx, parts):
    return pl.pallas_call(
        pick_kernel,
        grid=(8,),
        in_specs=[pl.BlockSpec(memory_space=SMEM)] * 2 + [pl.BlockSpec(memory_space=pl.ANY)] * 16,
        out_specs=[pl.BlockSpec(memory_space=pl.ANY)] * 2,
        out_shape=[jax.ShapeDtypeStruct((count, 4, 256, 512), BF16) for count in SPLIT],
        scratch_shapes=[
            VMEM((2048, 16, 128), BF16),
            VMEM((128, 1024), BF16),
            VMEM((2, 4, 256, 512), BF16),
            pltpu.SemaphoreType.DMA((16,)),
            pltpu.SemaphoreType.DMA((2,)),
        ],
        cost_estimate=pl.CostEstimate(
            flops=2 * 32 * 128 * 128 * 1024, bytes_accessed=18 << 20, transcendentals=0
        ),
        compiler_params=limit(16),
        name="pick",
    )(me, idx, *parts)


def q_kernel(start, count, phase_ref, data_ref, o0, o1, o2, o3, data, phase, sems, phase_sem):
    outs = (o0, o1, o2, o3)
    load_phase = pltpu.make_async_copy(phase_ref, phase, phase_sem)
    load_phase.start()

    def load(k, part):
        return pltpu.make_async_copy(
            data_ref.at[:, 2 * (start + k) + part], data.at[k, part], sems.at[k, part]
        )

    for k in range(count):
        for part in range(2):
            load(k, part).start()
    load_phase.wait()
    for k in range(count):
        if k % 2 == 0:
            for later in range(k, min(k + 2, count)):
                for part in range(2):
                    load(later, part).wait()
        stacked = data[k].reshape(1024, 256)
        result = jnp.dot(phase[...], stacked, preferred_element_type=F32).astype(BF16)
        for part in range(2):
            for bd in range(4):
                at = (part * 4 + bd) * 32
                outs[bd][k, part] = result[at : at + 32]


def q_transform(start, count, phase, data):
    whole = pl.BlockSpec(memory_space=VMEM)
    return pl.pallas_call(
        functools.partial(q_kernel, start, count),
        in_specs=[pl.BlockSpec(memory_space=pl.ANY)] * 2,
        out_specs=[whole] * 4,
        out_shape=[jax.ShapeDtypeStruct((count, 2, 32, 256), BF16)] * 4,
        scratch_shapes=[
            VMEM((count, 2, 32, 16, 256), BF16),
            VMEM((256, 1024), BF16),
            pltpu.SemaphoreType.DMA((count, 2)),
            pltpu.SemaphoreType.DMA,
        ],
        cost_estimate=pl.CostEstimate(
            flops=2 * count * 256 * 1024 * 256, bytes_accessed=3 << 20, transcendentals=0
        ),
        compiler_params=limit(12),
    )(phase, data)


def rotate_kernel(eig_ref, w0, w1, a0, a1, a2, a3, out_ref, even, odd, merged, done):
    start, count = 0, 8
    arrays = (a0, a1, a2, a3)
    quarter = lax.broadcasted_iota(jnp.int32, (8, 128), 1) // 32

    def first(k, halves):
        columns = []
        for part in range(2):
            whole = jnp.concatenate([ref[k, part] for ref in arrays], 0)
            columns.append((whole[:, 0:128], whole[:, 128:256]))
        both = jnp.concatenate(
            [jnp.concatenate([columns[0][hi], columns[1][hi]], 1) for hi in range(2)], 0
        )
        for low in range(4):
            blocks = []
            for part in range(2):
                for at in range(4):
                    block = eig_ref[k + start, part * 32 : part * 32 + 32]
                    blocks.append(block if at == low else jnp.zeros_like(block))
            half = jnp.dot(both, jnp.concatenate(blocks, 0), preferred_element_type=F32)
            for hi in range(2):
                for bd in range(4):
                    for group in range(4):
                        at = hi * 128 + bd * 32 + group * 8
                        place = (bd * 8 + hi * 4 + low) * 8
                        halves[group, place : place + 8] = half[at : at + 8, 0:128]
                        halves[group, 256 + place : 264 + place] = half[at : at + 8, 128:256]

    def second(k, halves):
        for group in range(4):
            rotated = jnp.dot(
                (w0, w1)[k // 4][k % 4, group], halves[group].astype(BF16), preferred_element_type=F32
            )
            square = rotated * rotated
            square = square + pltpu.roll(square, 32, 1)
            for m in range(8):
                parts = [square[(4 * m + mm) * 8 : (4 * m + mm) * 8 + 8] for mm in range(4)]
                merged[group * 8 : group * 8 + 8, m * 128 : m * 128 + 128] = jnp.where(
                    quarter == 0,
                    parts[0],
                    jnp.where(
                        quarter == 1, parts[1], jnp.where(quarter == 2, parts[2], parts[3])
                    ),
                )
        done[k] = merged[...].astype(BF16)

    slots = (even, odd)
    first(0, even)
    for k in range(count):
        if k + 1 < count:
            first(k + 1, slots[(k + 1) % 2])
        second(k, slots[k % 2])
    out_ref[...] = jnp.swapaxes(done[...], 0, 1)


def rotate(eig, picked, arrays):
    whole = pl.BlockSpec(memory_space=VMEM)
    return pl.pallas_call(
        rotate_kernel,
        in_specs=[whole] * 7,
        out_specs=whole,
        out_shape=jax.ShapeDtypeStruct((32, 8, 1024), BF16),
        scratch_shapes=[
            VMEM((4, 512, 128), F32),
            VMEM((4, 512, 128), F32),
            VMEM((32, 1024), F32),
            VMEM((8, 32, 1024), BF16),
        ],
        cost_estimate=pl.CostEstimate(
            flops=2 * 8 * 4 * (256 * 256 * 256 + 256 * 512 * 128),
            bytes_accessed=12 << 20,
            transcendentals=0,
        ),
        compiler_params=limit(10),
        name="rotate",
    )(eig, *picked, *arrays)


def shards(g_wannier, k_angle, q_angle, eig_k, eig_kq, mask_k, mask_kq, owner, kq_local):
    row = lax.axis_index("row")
    b = lax.axis_index("blk")
    z, x, c = row // 8, (row // 2) % 4, row % 2
    me = jnp.stack([z, x, c, b]).astype(jnp.int32)

    table = table_of(eig_kq, mask_kq)
    table, k_angle = lax.optimization_barrier((table, k_angle))
    from_x = []
    for d in (1, 2, 3):
        from_x.append(row_shift(table, dx=-d))
    along_x = jnp.stack([table] + from_x)
    from_z = []
    for d in (1, 2, 3):
        from_z.append(row_shift(along_x, dz=-d))
    halves = (jnp.stack([along_x, from_z[0]]), jnp.stack(from_z[1:]))
    own = {(0, 0): halves[0], (0, 1): halves[1]}
    for y, half, dy in ((1, 0, -1), (3, 1, 1), (1, 1, -1), (3, 0, 1)):
        own[y, half] = blk_shift(halves[half], dy)
    own[2, 0] = blk_shift(own[1, 0], -1)
    own[2, 1] = blk_shift(own[3, 1], 1)
    order = [(y, half) for y in range(4) for half in range(2)]
    parts = [own[at] for at in order]
    for y, half in order:
        parts.append(row_shift(own[y, half], dc=1))
    parts = [part.reshape(-1, 16, 128) for part in parts]

    own_row = owner.reshape(8, 32) // 4
    c_off = (own_row - c) % 2
    y_off = (owner.reshape(8, 32) - b) % 4
    z_off = (own_row // 8 - z) % 4
    x_off = (own_row // 2 - x) % 4
    idx = (((c_off * 4 + y_off) * 4 + z_off) * 4 + x_off) * 16 + kq_local.reshape(8, 32)

    k_phase = k_phase_of(k_angle)
    sent = k_transform(0, 8, k_phase, g_wannier)
    taken = lax.all_to_all(sent, "row", split_axis=0, concat_axis=0, tiled=True)

    phase, eig = prep(me, q_angle, eig_k, mask_k)
    picked = pick(me, idx, parts)
    outs = q_transform(0, 8, phase, taken)
    arrays = {0: outs[0]}
    for d in (1, 2, 3):
        arrays[(-d) % 4] = blk_shift(outs[d], d)
    return rotate(eig, picked, [arrays[off] for off in range(4)])


def solution(mesh):
    placed = (
        P("row", None, None, "blk"),
        P(),
        P(),
        P("row", None, None, None),
        P(("row", "blk"), None, None, None),
        P("row", None),
        P(("row", "blk"), None),
        P("blk", "row", None, None),
        P("blk", "row", None, None),
    )

    return jax.shard_map(
        shards, mesh=mesh, in_specs=placed, out_specs=P("blk", "row", None), check_vma=False
    )
```
